32 devices in a mesh: energy: 16 (over z, y, x), slab: 2 (over core).
Axes of the slice: x: 2, y: 2, z: 4, core: 2. Of those that a mesh axis runs over, the one named last changes fastest.
Arguments:
- green_ret: bfloat16 [48, 4, 3, 2, 192, 192], P('energy', 'slab'), may hold values from -0.3125 to 0.3125
- sigma_less: bfloat16 [48, 4, 2, 192, 192], P('energy', 'slab'), may hold values from -6 to 6
- screened: float32 [48, 4, 2, 36864], P(None, 'slab', None, 'energy'), may hold values from -4 to 4
Outputs:
- sigma_new: bfloat16 [48, 4, 2, 192, 192], P('energy', 'slab')
- renewed: bfloat16 [48, 4, 2, 192, 192], P('energy', 'slab')
The draws below stay inside these ranges and needn't reach their ends.
All inputs are finite; a program needn't handle non-finite values.
Results may differ from the reference program's by a relative error of at most 0.0085.
Values may be sent and summed in bfloat16 or wider, within the bound.
No kernel may reach another device: no remote copies, remote signals or barrier semaphores. Data moves between devices by JAX's collectives and lax.ppermute only.
A program may use at most 128 MiB of HBM per device.

```python
import math
import jax
import jax.numpy as jnp
from jax import lax

B = 192
E = 48
S = 4


def block_levels(key, dims, split, low, high):
    gain, own = 1.0, jax.random.fold_in(key, 6)
    for axis_at, blocks in split:
        draws = jnp.exp(jax.random.uniform(jax.random.fold_in(own, axis_at), (blocks,), jnp.float32, low / len(split), high / len(split)))
        gain = gain * jnp.repeat(draws, dims[axis_at] // blocks).reshape([-1 if axis == axis_at else 1 for axis in range(len(dims))])
    return gain


def scatter_about(key, extent, spread, reach, split=(), held_as=jnp.bfloat16):
    level = block_levels(key, extent, split, -0.22, 0.18) if split else 1.0
    entries = jax.random.normal(key, extent, jnp.float32) * spread * level
    return jnp.minimum(jnp.maximum(entries, -reach), reach).astype(held_as)


def setup_inputs(seed: int = 0) -> dict:
    streams_of = jax.random.split(jax.random.key(seed), 4)
    green_ret = scatter_about(streams_of[0], (E, S, 3, 2, B, B), (2 * B) ** -0.5, 0.3125, ((0, 16), (1, 2)))
    sigma_less = scatter_about(streams_of[1], (E, S, 2, B, B), 1.0, 6.0, ((0, 16), (1, 2)))
    screened = scatter_about(streams_of[2], (E, S, 2, B * B), 0.5, 4.0, ((1, 2), (3, 16)), jnp.float32)
    return dict(green_ret=green_ret, sigma_less=sigma_less, screened=screened)


def cmul_adj(left, right):
    lr = left[..., 0, :, :].astype(jnp.float32)
    li = left[..., 1, :, :].astype(jnp.float32)
    rr = right[..., 0, :, :].astype(jnp.float32)
    ri = right[..., 1, :, :].astype(jnp.float32)
    real = jnp.einsum('...ab,...cb->...ac', lr, rr) + jnp.einsum('...ab,...cb->...ac', li, ri)
    imag = jnp.einsum('...ab,...cb->...ac', li, rr) - jnp.einsum('...ab,...cb->...ac', lr, ri)
    return jnp.stack([real, imag], axis=-3)

def cmul_plain(left, right):
    lr = left[..., 0, :, :].astype(jnp.float32)
    li = left[..., 1, :, :].astype(jnp.float32)
    rr = right[..., 0, :, :].astype(jnp.float32)
    ri = right[..., 1, :, :].astype(jnp.float32)
    real = jnp.einsum('...ab,...bc->...ac', lr, rr) - jnp.einsum('...ab,...bc->...ac', li, ri)
    imag = jnp.einsum('...ab,...bc->...ac', lr, ri) + jnp.einsum('...ab,...bc->...ac', li, rr)
    return jnp.stack([real, imag], axis=-3)

def reference(green_ret, sigma_less, screened):

    def congruence(pair):
        blocks, sigma = pair
        padded = jnp.pad(sigma, ((1, 1), (0, 0), (0, 0), (0, 0)))
        total = jnp.zeros(sigma.shape, jnp.float32)
        for k in range(3):
            coupling = blocks[:, k]
            inner = cmul_adj(padded[k:k + S], coupling).astype(jnp.bfloat16)
            total = total + cmul_plain(coupling, inner)
        return total.astype(jnp.bfloat16)
    lesser = lax.map(congruence, (green_ret, sigma_less))
    flat = lesser.astype(jnp.float32).reshape(E, S, 2, B * B)
    gcomp = flat[:, :, 0] + 1j * flat[:, :, 1]
    wcomp = screened[:, :, 0] + 1j * screened[:, :, 1]
    conv = jnp.fft.ifft(jnp.fft.fft(gcomp, axis=0) * jnp.fft.fft(wcomp, axis=0), axis=0) / math.sqrt(E)
    sigma_new = jnp.stack([conv.real, conv.imag], axis=2).reshape(E, S, 2, B, B).astype(jnp.bfloat16)

    def second(pair):
        blocks, fresh = pair
        diag = blocks[:, 1]
        inner = cmul_adj(fresh, diag).astype(jnp.bfloat16)
        return cmul_plain(diag, inner).astype(jnp.bfloat16)
    renewed = lax.map(second, (green_ret, sigma_new))
    return (sigma_new, renewed)
```

```python
import functools
import math

import jax
import jax.numpy as jnp
import ml_dtypes
import numpy as np
from jax import lax
from jax.experimental import pallas as pl
from jax.experimental.pallas import tpu as pltpu
from jax.sharding import PartitionSpec as P

LANES = 128
NT = (((1,), (1,)), ((), ()))
NN = (((1,), (0,)), ((), ()))


def dot(left, right, dims):
    return lax.dot_general(left, right, dims, preferred_element_type=jnp.float32)


def congruence(green, sigma):
    order = green.shape[-1]
    both = sigma.reshape(2 * order, order)
    by_real = dot(both, green[0], NT)
    by_imag = dot(both, green[1], NT)
    inner_real = (by_real[:order] + by_imag[order:]).astype(jnp.bfloat16)
    inner_imag = (by_real[order:] - by_imag[:order]).astype(jnp.bfloat16)
    stacked = green.reshape(2 * order, order)
    on_real = dot(stacked, inner_real, NN)
    on_imag = dot(stacked, inner_imag, NN)
    return on_real[:order] - on_imag[order:], on_imag[:order] + on_real[order:]


def lesser_kernel(green_ref, sigma_ref, halo_ref, out_ref, stage):
    order = green_ref.shape[-1]
    rest = order - LANES
    first = lax.axis_index("slab") == 0
    halo_slab = jnp.where(first, 1, 0)
    halo_block = jnp.where(first, 2, 0)
    far = congruence(green_ref[0, halo_slab, halo_block], halo_ref[0, 0])
    totals = []
    for slab in range(2):
        keep = halo_slab == slab
        total = [jnp.where(keep, part, 0.0) for part in far]
        for source in range(2):
            term = congruence(green_ref[0, slab, source - slab + 1], sigma_ref[0, source])
            total = [sum_ + new for sum_, new in zip(total, term)]
        totals.append(total)
    for part in range(2):
        one, two = totals[0][part], totals[1][part]
        rows = pl.ds(part, order, stride=2)
        stage[0, rows, :] = one[:, :LANES]
        stage[1, rows, :] = two[:, :LANES]
        stage[2, rows, :] = jnp.concatenate([one[:, LANES:], two[:, LANES:]], axis=1)
    devices, blocks, depth, _ = out_ref.shape
    for block in range(blocks):
        out_ref[:, block] = stage[block].reshape(devices, depth, LANES).astype(jnp.bfloat16)


def convolve_kernel(got_ref, what_ref, fwd_ref, bwd_ref, out_ref, stage, packed):
    devices, _, rows, _ = got_ref.shape
    half = packed.shape[0] // 2
    local = half // devices
    depth = rows // local
    owned = depth // 2
    stage[...] = got_ref[:, 0].astype(jnp.float32).reshape(devices * rows, LANES)
    for row in range(owned):
        for part in range(2):
            for energy in range(local):
                picked = stage[pl.ds(energy * depth + row * 2 + part, devices, stride=rows), :]
                at = part * half + energy * devices
                packed[at : at + devices, row * LANES : (row + 1) * LANES] = picked.astype(jnp.bfloat16)
    held = packed[...]
    ghat = dot(fwd_ref[0], held, NN) + dot(fwd_ref[1], held, NN)
    what = what_ref[0]
    real = ghat[:half] * what[:half] - ghat[half:] * what[half:]
    imag = ghat[:half] * what[half:] + ghat[half:] * what[:half]
    product = jnp.concatenate([real, imag], axis=0)
    high = product.astype(jnp.bfloat16)
    low = (product - high.astype(jnp.float32)).astype(jnp.bfloat16)
    result = dot(bwd_ref[0], high, NN) + dot(bwd_ref[1], high, NN) + dot(bwd_ref[0], low, NN)
    for row in range(owned):
        for part in range(2):
            for energy in range(local):
                at = part * half + energy * devices
                stage[pl.ds(energy * depth + row * 2 + part, devices, stride=rows), :] = result[
                    at : at + devices, row * LANES : (row + 1) * LANES
                ]
    out_ref[:, 0] = stage[...].reshape(devices, rows, LANES).astype(jnp.bfloat16)


def renew_kernel(got_ref, green_ref, sigma_ref, renewed_ref, stage):
    order = green_ref.shape[-1]
    rest = order - LANES
    for block in range(3):
        stage[block] = got_ref[:, block].astype(jnp.float32).reshape(2 * order, LANES)
    for part in range(2):
        rows = pl.ds(part, order, stride=2)
        one = stage[0, rows, :].astype(jnp.bfloat16)
        two = stage[1, rows, :].astype(jnp.bfloat16)
        mixed = stage[2, rows, :]
        sigma_ref[0, 0, part, :, :LANES] = one
        sigma_ref[0, 1, part, :, :LANES] = two
        sigma_ref[0, 0, part, :, LANES:] = mixed[:, :rest].astype(jnp.bfloat16)
        sigma_ref[0, 1, part, :, LANES:] = pltpu.roll(mixed, rest, 1)[:, :rest].astype(jnp.bfloat16)
    for slab in range(2):
        real, imag = congruence(green_ref[0, slab, 0], sigma_ref[0, slab])
        renewed_ref[0, slab, 0] = real.astype(jnp.bfloat16)
        renewed_ref[0, slab, 1] = imag.astype(jnp.bfloat16)


def split_high_low(matrix):
    high = matrix.astype(ml_dtypes.bfloat16)
    low = (matrix - high.astype(np.float64)).astype(ml_dtypes.bfloat16)
    return jnp.asarray(np.stack([high, low]))


def transforms(energies, devices):
    local = energies // devices
    index = np.arange(energies)
    angle = (index[:, None] * index[None, :] % energies) * (2.0 * math.pi / energies)
    cosine, sine = np.cos(angle), np.sin(angle)
    order = (np.arange(devices)[None, :] * local + np.arange(local)[:, None]).reshape(-1)
    scale = 1.0 / (energies * math.sqrt(energies))
    forward = np.block([[cosine[:, order], sine[:, order]], [-sine[:, order], cosine[:, order]]])
    backward = scale * np.block([[cosine[order], -sine[order]], [sine[order], cosine[order]]])
    plain = np.stack([np.stack([cosine, sine], 1), np.stack([-sine, cosine], 1)])
    return split_high_low(forward), split_high_low(backward), jnp.asarray(plain, jnp.float32)


def fast_shards(green_ret, sigma_less, screened):
    devices = lax.axis_size("energy")
    local, slabs, _, order, _ = sigma_less.shape
    energies = local * devices
    owned = order // devices
    depth = 2 * owned
    rows = depth * local
    rest = order - LANES

    edge = 1 - lax.axis_index("slab")
    halo = lax.ppermute(
        lax.dynamic_slice_in_dim(sigma_less, edge, 1, axis=1), "slab", [(0, 1), (1, 0)]
    )
    zeros = (0,) * 5
    send = pl.pallas_call(
        lesser_kernel,
        out_shape=jax.ShapeDtypeStruct((devices, 3, rows, LANES), jnp.bfloat16),
        grid=(local,),
        in_specs=[
            pl.BlockSpec((1, slabs, 3, 2, order, order), lambda e: (e, 0, 0, 0, 0, 0)),
            pl.BlockSpec((1, slabs, 2, order, order), lambda e: (e, 0, 0, 0, 0)),
            pl.BlockSpec((1, 1, 2, order, order), lambda e: (e, 0, 0, 0, 0)),
        ],
        out_specs=pl.BlockSpec((devices, 3, depth, LANES), lambda e: (0, 0, e, 0)),
        scratch_shapes=[pltpu.VMEM((3, 2 * order, LANES), jnp.float32)],
        name="lesser",
    )(green_ret, sigma_less, halo)
    got = lax.all_to_all(send, "energy", split_axis=0, concat_axis=0, tiled=True)

    forward, backward, plain = transforms(energies, devices)
    grid_w = screened.reshape(energies, slabs, 2, owned, order)
    head, tail = grid_w[..., :LANES], grid_w[..., LANES:]
    arranged = jnp.stack([head[:, 0], head[:, 1], jnp.concatenate([tail[:, 0], tail[:, 1]], axis=-1)])
    arranged = arranged.reshape(3, energies, 2, owned * LANES)
    what = jnp.einsum("pfqe,keqn->kpfn", plain, arranged, precision=lax.Precision.HIGH)
    what = what.reshape(3, 2 * energies, owned * LANES)

    fresh = pl.pallas_call(
        convolve_kernel,
        out_shape=jax.ShapeDtypeStruct((devices, 3, rows, LANES), jnp.bfloat16),
        grid=(3,),
        in_specs=[
            pl.BlockSpec((devices, 1, rows, LANES), lambda k: (0, k, 0, 0)),
            pl.BlockSpec((1, 2 * energies, owned * LANES), lambda k: (k, 0, 0)),
            pl.BlockSpec((2, 2 * energies, 2 * energies), lambda k: (0, 0, 0)),
            pl.BlockSpec((2, 2 * energies, 2 * energies), lambda k: (0, 0, 0)),
        ],
        out_specs=pl.BlockSpec((devices, 1, rows, LANES), lambda k: (0, k, 0, 0)),
        scratch_shapes=[
            pltpu.VMEM((devices * rows, LANES), jnp.float32),
            pltpu.VMEM((2 * energies, owned * LANES), jnp.bfloat16),
        ],
        name="convolve",
    )(got, what, forward, backward)
    back = lax.all_to_all(fresh, "energy", split_axis=0, concat_axis=0, tiled=True)

    out = jax.ShapeDtypeStruct((local, slabs, 2, order, order), jnp.bfloat16)
    whole_block = pl.BlockSpec((1, slabs, 2, order, order), lambda e: (e, 0, 0, 0, 0))
    return pl.pallas_call(
        renew_kernel,
        out_shape=(out, out),
        grid=(local,),
        in_specs=[
            pl.BlockSpec((devices, 3, depth, LANES), lambda e: (0, 0, e, 0)),
            pl.BlockSpec((1, slabs, 1, 2, order, order), lambda e: (e, 0, 1, 0, 0, 0)),
        ],
        out_specs=(whole_block, whole_block),
        scratch_shapes=[pltpu.VMEM((3, 2 * order, LANES), jnp.float32)],
        name="renew",
    )(back, green_ret)


def with_halo(cells, sides, width):
    for axis, dim in sides:
        count = lax.axis_size(axis)
        ends = count - 1
        head = lax.slice_in_dim(cells, 0, width, axis=dim)
        tail = lax.slice_in_dim(cells, cells.shape[dim] - width, cells.shape[dim], axis=dim)
        cells = jnp.concatenate(
            [
                lax.ppermute(tail, axis, [(i, (i + 1) % count) for i in range(ends)]),
                cells,
                lax.ppermute(head, axis, [((i + 1) % count, i) for i in range(ends)]),
            ],
            axis=dim,
        )
    return cells


def cmul_adj(left, right):
    lr = left[..., 0, :, :]
    li = left[..., 1, :, :]
    rr = right[..., 0, :, :]
    ri = right[..., 1, :, :]
    real = jnp.einsum(
        "...ab,...cb->...ac", lr, rr, preferred_element_type=jnp.float32
    ) + jnp.einsum("...ab,...cb->...ac", li, ri, preferred_element_type=jnp.float32)
    imag = jnp.einsum(
        "...ab,...cb->...ac", li, rr, preferred_element_type=jnp.float32
    ) - jnp.einsum("...ab,...cb->...ac", lr, ri, preferred_element_type=jnp.float32)
    return jnp.stack([real, imag], axis=-3)


def cmul_plain(left, right):
    lr = left[..., 0, :, :]
    li = left[..., 1, :, :]
    rr = right[..., 0, :, :]
    ri = right[..., 1, :, :]
    real = jnp.einsum(
        "...ab,...bc->...ac", lr, rr, preferred_element_type=jnp.float32
    ) - jnp.einsum("...ab,...bc->...ac", li, ri, preferred_element_type=jnp.float32)
    imag = jnp.einsum(
        "...ab,...bc->...ac", lr, ri, preferred_element_type=jnp.float32
    ) + jnp.einsum("...ab,...bc->...ac", li, rr, preferred_element_type=jnp.float32)
    return jnp.stack([real, imag], axis=-3)


def convolve(owned, interaction):
    energies = owned.shape[0]
    index = jnp.arange(energies, dtype=jnp.int32)
    phase = index[:, None] * index[None, :] % energies
    angle = phase.astype(jnp.float32) * (2.0 * math.pi / energies)
    cosine = jnp.cos(angle)
    sine = jnp.sin(angle)
    forward = jnp.stack(
        [jnp.stack([cosine, sine], axis=1), jnp.stack([-sine, cosine], axis=1)], axis=0
    )
    backward = jnp.stack(
        [jnp.stack([cosine, -sine], axis=1), jnp.stack([sine, cosine], axis=1)], axis=0
    )
    ghat = jnp.einsum(
        "pfqe,esqn->pfsn", forward, owned.astype(jnp.float32), precision=lax.Precision.HIGH
    )
    what = jnp.einsum("pfqe,esqn->pfsn", forward, interaction, precision=lax.Precision.HIGH)
    prod_real = ghat[0] * what[0] - ghat[1] * what[1]
    prod_imag = ghat[0] * what[1] + ghat[1] * what[0]
    product = jnp.stack([prod_real, prod_imag], axis=0)
    result = jnp.einsum("pfqe,qesn->fspn", backward, product, precision=lax.Precision.HIGH)
    result = result * (1.0 / (energies * math.sqrt(energies)))
    return result.astype(jnp.bfloat16)


def plain_shards(green_ret, sigma_less, screened):
    energy_dev = sigma_less.shape[0]
    slab_dev = sigma_less.shape[1]
    order = sigma_less.shape[-1]
    padded = with_halo(sigma_less, (("slab", 1),), 1)
    total = None
    for k in range(3):
        coupling = green_ret[:, :, k]
        inner = cmul_adj(padded[:, k : k + slab_dev], coupling).astype(jnp.bfloat16)
        term = cmul_plain(coupling, inner)
        total = term if total is None else total + term
    lesser = total.astype(jnp.bfloat16).reshape(energy_dev, slab_dev, 2, order * order)
    owned = lax.all_to_all(lesser, "energy", split_axis=3, concat_axis=0, tiled=True)
    fresh = convolve(owned, screened)
    sigma_new = lax.all_to_all(fresh, "energy", split_axis=0, concat_axis=3, tiled=True)
    sigma_new = sigma_new.reshape(energy_dev, slab_dev, 2, order, order)
    diag = green_ret[:, :, 1]
    inner = cmul_adj(sigma_new, diag).astype(jnp.bfloat16)
    renewed = cmul_plain(diag, inner).astype(jnp.bfloat16)
    return (sigma_new, renewed)


def shards(green_ret, sigma_less, screened):
    order = sigma_less.shape[-1]
    devices = lax.axis_size("energy")
    fits = (
        lax.axis_size("slab") == 2
        and sigma_less.shape[1] == 2
        and order == LANES + LANES // 2
        and order % devices == 0
        and (2 * order // devices) % 8 == 0
        and devices % 16 == 0
    )
    return (fast_shards if fits else plain_shards)(green_ret, sigma_less, screened)


def solution(mesh):
    in_specs = (
        P("energy", "slab", None, None, None, None),
        P("energy", "slab", None, None, None),
        P(None, "slab", None, "energy"),
    )
    out_specs = (P("energy", "slab", None, None, None), P("energy", "slab", None, None, None))
    return jax.shard_map(shards, mesh=mesh, in_specs=in_specs, out_specs=out_specs, check_vma=False)
```

```python
import functools
import math

import jax
import jax.numpy as jnp
import ml_dtypes
import numpy as np
from jax import lax
from jax.experimental import pallas as pl
from jax.experimental.pallas import tpu as pltpu
from jax.sharding import PartitionSpec as P

LANES = 128
NT = (((1,), (1,)), ((), ()))
NN = (((1,), (0,)), ((), ()))


def dot(left, right, dims):
    return lax.dot_general(left, right, dims, preferred_element_type=jnp.float32)


def inner_parts(green, sigma):
    real = dot(sigma[0], green[0], NT) + dot(sigma[1], green[1], NT)
    imag = dot(sigma[1], green[0], NT) + dot(sigma[0], -green[1], NT)
    return real.astype(jnp.bfloat16), imag.astype(jnp.bfloat16)


def outer_parts(green, inner):
    real, imag = inner
    return (
        dot(green[0], real, NN) + dot(-green[1], imag, NN),
        dot(green[0], imag, NN) + dot(green[1], real, NN),
    )


def congruence(green, sigma):
    return outer_parts(green, inner_parts(green, sigma))


def edge_place(slab_axis):
    first = lax.axis_index(slab_axis) == 0
    return jnp.where(first, 1, 0), jnp.where(first, 2, 0)


def near_kernel(green_hbm, sigma_hbm, total_ref, edge_ref, green, sigma, sems):
    local = green.shape[0]
    edge_slab, edge_block = edge_place("slab")
    copies = []
    for energy in range(local):
        copies.append(
            [
                pltpu.make_async_copy(sigma_hbm.at[energy], sigma.at[energy], sems.at[energy, 0]),
                pltpu.make_async_copy(
                    green_hbm.at[energy, 0, pl.ds(1, 2)], green.at[energy, 0], sems.at[energy, 1]
                ),
                pltpu.make_async_copy(
                    green_hbm.at[energy, 1, pl.ds(0, 2)], green.at[energy, 1], sems.at[energy, 2]
                ),
            ]
        )
    edges = [
        pltpu.make_async_copy(
            green_hbm.at[energy, edge_slab, edge_block], edge_ref.at[energy], sems.at[energy, 3]
        )
        for energy in range(local)
    ]
    for group in copies:
        for copy in group:
            copy.start()
    for copy in edges:
        copy.start()
    for energy in range(local):
        for copy in copies[energy]:
            copy.wait()
        for slab in range(2):
            terms = [
                congruence(green[energy, slab, source], sigma[energy, source]) for source in range(2)
            ]
            for part in range(2):
                total_ref[energy, slab, part] = terms[0][part] + terms[1][part]
    for copy in edges:
        copy.wait()


def far_kernel(total_ref, edge_ref, halo_ref, out_ref, stage):
    local, _, _, order, _ = total_ref.shape
    devices, blocks, rows, _ = out_ref.shape
    depth = rows // local
    edge_slab, _ = edge_place("slab")
    other = 1 - edge_slab
    for energy in range(local):
        far = congruence(edge_ref[energy], halo_ref[energy, other])
        for part in range(2):
            one, two = [
                total_ref[energy, slab, part] + jnp.where(edge_slab == slab, far[part], 0.0)
                for slab in range(2)
            ]
            at = pl.ds(part, order, stride=2)
            stage[energy, 0, at, :] = one[:, :LANES]
            stage[energy, 1, at, :] = two[:, :LANES]
            stage[energy, 2, at, :] = jnp.concatenate([one[:, LANES:], two[:, LANES:]], axis=1)
        for block in range(blocks):
            out_ref[:, block, energy * depth : (energy + 1) * depth] = (
                stage[energy, block].reshape(devices, depth, LANES).astype(jnp.bfloat16)
            )


def convolve_kernel(got_ref, what_ref, fwd_ref, bwd_ref, out_ref, stage, packed):
    devices, blocks, rows, _ = got_ref.shape
    half = fwd_ref.shape[0] // 2
    local = half // devices
    depth = rows // local
    owned = depth // 2
    for block in range(blocks):
        flat = stage.at[block]
        flat[...] = got_ref[:, block].astype(jnp.float32).reshape(devices * rows, LANES)
        for row in range(owned):
            for part in range(2):
                for energy in range(local):
                    picked = flat[pl.ds(energy * depth + row * 2 + part, devices, stride=rows), :]
                    at = part * half + energy * devices
                    packed[block, at : at + devices, row * LANES : (row + 1) * LANES] = picked.astype(
                        jnp.bfloat16
                    )
        held = packed[block]
        ghat = dot(fwd_ref[...], jnp.concatenate([held, held], axis=0), NN)
        what = what_ref[block]
        real = ghat[:half] * what[:half] - ghat[half:] * what[half:]
        imag = ghat[:half] * what[half:] + ghat[half:] * what[:half]
        product = jnp.concatenate([real, imag], axis=0).astype(jnp.bfloat16)
        result = dot(bwd_ref[...], jnp.concatenate([product, product], axis=0), NN)
        for row in range(owned):
            for part in range(2):
                for energy in range(local):
                    at = part * half + energy * devices
                    flat[pl.ds(energy * depth + row * 2 + part, devices, stride=rows), :] = result[
                        at : at + devices, row * LANES : (row + 1) * LANES
                    ]
        out_ref[:, block] = flat[...].reshape(devices, rows, LANES).astype(jnp.bfloat16)


def renew_kernel(got_ref, green_ref, sigma_hbm, renewed_hbm, stage, sigma, renewed, sems):
    local, _, _, order, _ = sigma.shape
    rows = got_ref.shape[2]
    depth = rows // local
    rest = order - LANES
    copies = []
    for energy in range(local):
        for block in range(3):
            stage[energy, block] = (
                got_ref[:, block, energy * depth : (energy + 1) * depth]
                .astype(jnp.float32)
                .reshape(2 * order, LANES)
            )
        for part in range(2):
            at = pl.ds(part, order, stride=2)
            mixed = stage[energy, 2, at, :]
            sigma[energy, 0, part, :, :LANES] = stage[energy, 0, at, :].astype(jnp.bfloat16)
            sigma[energy, 1, part, :, :LANES] = stage[energy, 1, at, :].astype(jnp.bfloat16)
            sigma[energy, 0, part, :, LANES:] = mixed[:, :rest].astype(jnp.bfloat16)
            sigma[energy, 1, part, :, LANES:] = pltpu.roll(mixed, rest, 1)[:, :rest].astype(jnp.bfloat16)
        copies.append(pltpu.make_async_copy(sigma.at[energy], sigma_hbm.at[energy], sems.at[energy, 0]))
        copies[-1].start()
        for slab in range(2):
            fresh = congruence(green_ref[energy, slab, 0], sigma[energy, slab])
            for part in range(2):
                renewed[energy, slab, part] = fresh[part].astype(jnp.bfloat16)
            copies.append(
                pltpu.make_async_copy(
                    renewed.at[energy, slab], renewed_hbm.at[energy, slab], sems.at[energy, 1 + slab]
                )
            )
            copies[-1].start()
    for copy in copies:
        copy.wait()


def split_high_low(matrix):
    high = matrix.astype(ml_dtypes.bfloat16)
    low = (matrix - high.astype(np.float64)).astype(ml_dtypes.bfloat16)
    return jnp.asarray(np.concatenate([high, low], axis=1))


def transforms(energies, devices):
    local = energies // devices
    index = np.arange(energies)
    angle = (index[:, None] * index[None, :] % energies) * (2.0 * math.pi / energies)
    cosine, sine = np.cos(angle), np.sin(angle)
    order = (np.arange(devices)[None, :] * local + np.arange(local)[:, None]).reshape(-1)
    scale = 1.0 / (energies * math.sqrt(energies))
    forward = np.block([[cosine[:, order], sine[:, order]], [-sine[:, order], cosine[:, order]]])
    backward = scale * np.block([[cosine[order], -sine[order]], [sine[order], cosine[order]]])
    plain = np.stack([np.stack([cosine, sine], 1), np.stack([-sine, cosine], 1)])
    return split_high_low(forward), split_high_low(backward), jnp.asarray(plain, jnp.float32)


def vmem(array):
    return pltpu.with_memory_space_constraint(array, pltpu.VMEM)


def hbm(array):
    return pltpu.with_memory_space_constraint(array, pltpu.HBM)


IN_VMEM = pl.BlockSpec(memory_space=pltpu.VMEM)
IN_HBM = pl.BlockSpec(memory_space=pltpu.HBM)
GRANT = pltpu.CompilerParams(vmem_limit_bytes=20 << 20)


def fast_shards(green_ret, sigma_less, screened):
    devices = lax.axis_size("energy")
    local, slabs, _, order, _ = sigma_less.shape
    energies = local * devices
    owned = order // devices
    depth = 2 * owned
    rows = depth * local
    sent = pltpu.VMEM((devices, 3, rows, LANES), jnp.bfloat16)
    dma = pltpu.SemaphoreType.DMA

    halo = lax.ppermute(sigma_less, "slab", [(0, 1), (1, 0)])
    total, edge = pl.pallas_call(
        near_kernel,
        out_shape=(
            pltpu.VMEM((local, slabs, 2, order, order), jnp.float32),
            pltpu.VMEM((local, 2, order, order), jnp.bfloat16),
        ),
        in_specs=[IN_HBM, IN_HBM],
        out_specs=(IN_VMEM, IN_VMEM),
        scratch_shapes=[
            pltpu.VMEM((local, slabs, 2, 2, order, order), jnp.bfloat16),
            pltpu.VMEM((local, slabs, 2, order, order), jnp.bfloat16),
            dma((local, 4)),
        ],
        compiler_params=GRANT,
        name="near",
    )(hbm(green_ret), hbm(sigma_less))
    send = pl.pallas_call(
        far_kernel,
        out_shape=sent,
        in_specs=[IN_VMEM] * 3,
        out_specs=IN_VMEM,
        scratch_shapes=[pltpu.VMEM((local, 3, 2 * order, LANES), jnp.float32)],
        compiler_params=GRANT,
        name="far",
    )(vmem(total), vmem(edge), vmem(halo))
    got = lax.all_to_all(send, "energy", split_axis=0, concat_axis=0, tiled=True)

    forward, backward, plain = transforms(energies, devices)
    grid_w = screened.reshape(energies, slabs, 2, owned, order)
    head, tail = grid_w[..., :LANES], grid_w[..., LANES:]
    arranged = jnp.stack([head[:, 0], head[:, 1], jnp.concatenate([tail[:, 0], tail[:, 1]], axis=-1)])
    arranged = arranged.reshape(3, energies, 2, owned * LANES)
    what = jnp.einsum("pfqe,keqn->kpfn", plain, arranged, precision=lax.Precision.HIGH)
    what = what.reshape(3, 2 * energies, owned * LANES)

    fresh = pl.pallas_call(
        convolve_kernel,
        out_shape=sent,
        in_specs=[IN_VMEM] * 4,
        out_specs=IN_VMEM,
        scratch_shapes=[
            pltpu.VMEM((3, devices * rows, LANES), jnp.float32),
            pltpu.VMEM((3, 2 * energies, owned * LANES), jnp.bfloat16),
        ],
        compiler_params=GRANT,
        name="convolve",
    )(vmem(got), vmem(what), vmem(forward), vmem(backward))
    back = lax.all_to_all(fresh, "energy", split_axis=0, concat_axis=0, tiled=True)

    out = jax.ShapeDtypeStruct((local, slabs, 2, order, order), jnp.bfloat16)
    return pl.pallas_call(
        renew_kernel,
        out_shape=(out, out),
        in_specs=[IN_VMEM] * 2,
        out_specs=(IN_HBM, IN_HBM),
        scratch_shapes=[
            pltpu.VMEM((local, 3, 2 * order, LANES), jnp.float32),
            pltpu.VMEM((local, slabs, 2, order, order), jnp.bfloat16),
            pltpu.VMEM((local, slabs, 2, order, order), jnp.bfloat16),
            dma((local, 3)),
        ],
        compiler_params=GRANT,
        name="renew",
    )(vmem(back), vmem(green_ret[:, :, 1:2]))


def with_halo(cells, sides, width):
    for axis, dim in sides:
        count = lax.axis_size(axis)
        ends = count - 1
        head = lax.slice_in_dim(cells, 0, width, axis=dim)
        tail = lax.slice_in_dim(cells, cells.shape[dim] - width, cells.shape[dim], axis=dim)
        cells = jnp.concatenate(
            [
                lax.ppermute(tail, axis, [(i, (i + 1) % count) for i in range(ends)]),
                cells,
                lax.ppermute(head, axis, [((i + 1) % count, i) for i in range(ends)]),
            ],
            axis=dim,
        )
    return cells


def cmul_adj(left, right):
    lr = left[..., 0, :, :]
    li = left[..., 1, :, :]
    rr = right[..., 0, :, :]
    ri = right[..., 1, :, :]
    real = jnp.einsum(
        "...ab,...cb->...ac", lr, rr, preferred_element_type=jnp.float32
    ) + jnp.einsum("...ab,...cb->...ac", li, ri, preferred_element_type=jnp.float32)
    imag = jnp.einsum(
        "...ab,...cb->...ac", li, rr, preferred_element_type=jnp.float32
    ) - jnp.einsum("...ab,...cb->...ac", lr, ri, preferred_element_type=jnp.float32)
    return jnp.stack([real, imag], axis=-3)


def cmul_plain(left, right):
    lr = left[..., 0, :, :]
    li = left[..., 1, :, :]
    rr = right[..., 0, :, :]
    ri = right[..., 1, :, :]
    real = jnp.einsum(
        "...ab,...bc->...ac", lr, rr, preferred_element_type=jnp.float32
    ) - jnp.einsum("...ab,...bc->...ac", li, ri, preferred_element_type=jnp.float32)
    imag = jnp.einsum(
        "...ab,...bc->...ac", lr, ri, preferred_element_type=jnp.float32
    ) + jnp.einsum("...ab,...bc->...ac", li, rr, preferred_element_type=jnp.float32)
    return jnp.stack([real, imag], axis=-3)


def convolve(owned, interaction):
    energies = owned.shape[0]
    index = jnp.arange(energies, dtype=jnp.int32)
    phase = index[:, None] * index[None, :] % energies
    angle = phase.astype(jnp.float32) * (2.0 * math.pi / energies)
    cosine = jnp.cos(angle)
    sine = jnp.sin(angle)
    forward = jnp.stack(
        [jnp.stack([cosine, sine], axis=1), jnp.stack([-sine, cosine], axis=1)], axis=0
    )
    backward = jnp.stack(
        [jnp.stack([cosine, -sine], axis=1), jnp.stack([sine, cosine], axis=1)], axis=0
    )
    ghat = jnp.einsum(
        "pfqe,esqn->pfsn", forward, owned.astype(jnp.float32), precision=lax.Precision.HIGH
    )
    what = jnp.einsum("pfqe,esqn->pfsn", forward, interaction, precision=lax.Precision.HIGH)
    prod_real = ghat[0] * what[0] - ghat[1] * what[1]
    prod_imag = ghat[0] * what[1] + ghat[1] * what[0]
    product = jnp.stack([prod_real, prod_imag], axis=0)
    result = jnp.einsum("pfqe,qesn->fspn", backward, product, precision=lax.Precision.HIGH)
    result = result * (1.0 / (energies * math.sqrt(energies)))
    return result.astype(jnp.bfloat16)


def plain_shards(green_ret, sigma_less, screened):
    energy_dev = sigma_less.shape[0]
    slab_dev = sigma_less.shape[1]
    order = sigma_less.shape[-1]
    padded = with_halo(sigma_less, (("slab", 1),), 1)
    total = None
    for k in range(3):
        coupling = green_ret[:, :, k]
        inner = cmul_adj(padded[:, k : k + slab_dev], coupling).astype(jnp.bfloat16)
        term = cmul_plain(coupling, inner)
        total = term if total is None else total + term
    lesser = total.astype(jnp.bfloat16).reshape(energy_dev, slab_dev, 2, order * order)
    owned = lax.all_to_all(lesser, "energy", split_axis=3, concat_axis=0, tiled=True)
    fresh = convolve(owned, screened)
    sigma_new = lax.all_to_all(fresh, "energy", split_axis=0, concat_axis=3, tiled=True)
    sigma_new = sigma_new.reshape(energy_dev, slab_dev, 2, order, order)
    diag = green_ret[:, :, 1]
    inner = cmul_adj(sigma_new, diag).astype(jnp.bfloat16)
    renewed = cmul_plain(diag, inner).astype(jnp.bfloat16)
    return (sigma_new, renewed)


def shards(green_ret, sigma_less, screened):
    order = sigma_less.shape[-1]
    devices = lax.axis_size("energy")
    fits = (
        lax.axis_size("slab") == 2
        and sigma_less.shape[1] == 2
        and order == LANES + LANES // 2
        and order % devices == 0
        and (2 * order // devices) % 8 == 0
        and devices % 16 == 0
    )
    return (fast_shards if fits else plain_shards)(green_ret, sigma_less, screened)


def solution(mesh):
    in_specs = (
        P("energy", "slab", None, None, None, None),
        P("energy", "slab", None, None, None),
        P(None, "slab", None, "energy"),
    )
    out_specs = (P("energy", "slab", None, None, None), P("energy", "slab", None, None, None))
    return jax.shard_map(shards, mesh=mesh, in_specs=in_specs, out_specs=out_specs, check_vma=False)
```

```python
import functools
import math

import jax
import jax.numpy as jnp
import ml_dtypes
import numpy as np
from jax import lax
from jax.experimental import pallas as pl
from jax.experimental.pallas import tpu as pltpu
from jax.sharding import PartitionSpec as P

LANES = 128
NT = (((1,), (1,)), ((), ()))
NN = (((1,), (0,)), ((), ()))


def dot(left, right, dims):
    return lax.dot_general(left, right, dims, preferred_element_type=jnp.float32)


def inner_parts(green, sigma):
    real = dot(sigma[0], green[0], NT) + dot(sigma[1], green[1], NT)
    imag = dot(sigma[1], green[0], NT) + dot(sigma[0], -green[1], NT)
    return real.astype(jnp.bfloat16), imag.astype(jnp.bfloat16)


def outer_parts(green, inner):
    real, imag = inner
    return (
        dot(green[0], real, NN) + dot(-green[1], imag, NN),
        dot(green[0], imag, NN) + dot(green[1], real, NN),
    )


def congruence(green, sigma):
    return outer_parts(green, inner_parts(green, sigma))


def edge_place(slab_axis):
    first = lax.axis_index(slab_axis) == 0
    return jnp.where(first, 1, 0), jnp.where(first, 2, 0)


def near_kernel(green_hbm, sigma_hbm, total_ref, edge_ref, green, sigma, sems):
    local = green.shape[0]
    edge_slab, edge_block = edge_place("slab")
    copies = []
    for energy in range(local):
        copies.append(
            [
                pltpu.make_async_copy(sigma_hbm.at[energy], sigma.at[energy], sems.at[energy, 0]),
                pltpu.make_async_copy(
                    green_hbm.at[energy, 0, pl.ds(1, 2)], green.at[energy, 0], sems.at[energy, 1]
                ),
                pltpu.make_async_copy(
                    green_hbm.at[energy, 1, pl.ds(0, 2)], green.at[energy, 1], sems.at[energy, 2]
                ),
            ]
        )
    edges = [
        pltpu.make_async_copy(
            green_hbm.at[energy, edge_slab, edge_block], edge_ref.at[energy], sems.at[energy, 3]
        )
        for energy in range(local)
    ]
    for group in copies:
        for copy in group:
            copy.start()
    for copy in edges:
        copy.start()
    for energy in range(local):
        copies[energy][0].wait()
        inner = []
        for slab in range(2):
            copies[energy][1 + slab].wait()
            inner.append(
                [inner_parts(green[energy, slab, source], sigma[energy, source]) for source in range(2)]
            )
        for slab in range(2):
            one, two = green[energy, slab, 0], green[energy, slab, 1]
            near, next_ = inner[slab]
            total_ref[energy, slab, 0] = (
                dot(one[0], near[0], NN)
                + dot(two[0], next_[0], NN)
                + dot(-one[1], near[1], NN)
                + dot(-two[1], next_[1], NN)
            )
            total_ref[energy, slab, 1] = (
                dot(one[0], near[1], NN)
                + dot(two[0], next_[1], NN)
                + dot(one[1], near[0], NN)
                + dot(two[1], next_[0], NN)
            )
    for copy in edges:
        copy.wait()


def far_kernel(total_ref, edge_ref, halo_ref, out_ref, stage):
    local, _, _, order, _ = total_ref.shape
    devices, blocks, rows, _ = out_ref.shape
    depth = rows // local
    edge_slab, _ = edge_place("slab")
    other = 1 - edge_slab
    inner = [inner_parts(edge_ref[energy], halo_ref[energy, other]) for energy in range(local)]
    for energy in range(local):
        far = outer_parts(edge_ref[energy], inner[energy])
        for part in range(2):
            one, two = [
                total_ref[energy, slab, part] + jnp.where(edge_slab == slab, far[part], 0.0)
                for slab in range(2)
            ]
            at = pl.ds(part, order, stride=2)
            stage[energy, 0, at, :] = one[:, :LANES]
            stage[energy, 1, at, :] = two[:, :LANES]
            stage[energy, 2, at, :] = jnp.concatenate([one[:, LANES:], two[:, LANES:]], axis=1)
        for block in range(blocks):
            out_ref[:, block, energy * depth : (energy + 1) * depth] = (
                stage[energy, block].reshape(devices, depth, LANES).astype(jnp.bfloat16)
            )


def convolve_kernel(got_ref, what_ref, fwd_ref, bwd_ref, out_ref, stage, result):
    devices, blocks, rows, _ = got_ref.shape
    half = fwd_ref.shape[0] // 2
    local = half // devices
    depth = rows // local
    owned = depth // 2
    width = 2

    def place(block, row, part, energy):
        return block, pl.ds(energy * depth + row * 2 + part, devices, stride=rows), slice(None)

    each = [(part, energy) for part in range(2) for energy in range(local)]
    for block in range(blocks):
        stage[block] = got_ref[:, block].astype(jnp.float32).reshape(devices * rows, LANES)
        for start in range(0, owned, width):
            held = jnp.concatenate(
                [
                    jnp.concatenate([stage[place(block, row, *at)] for at in each], axis=0)
                    for row in range(start, start + width)
                ],
                axis=1,
            ).astype(jnp.bfloat16)
            ghat = dot(fwd_ref[...], jnp.concatenate([held, held], axis=0), NN)
            what = what_ref[block, :, start * LANES : (start + width) * LANES]
            real = ghat[:half] * what[:half] - ghat[half:] * what[half:]
            imag = ghat[:half] * what[half:] + ghat[half:] * what[:half]
            product = jnp.concatenate([real, imag], axis=0).astype(jnp.bfloat16)
            fresh = dot(bwd_ref[...], jnp.concatenate([product, product], axis=0), NN)
            for offset in range(width):
                for index, at in enumerate(each):
                    result[place(block, start + offset, *at)] = fresh[
                        index * devices : (index + 1) * devices, offset * LANES : (offset + 1) * LANES
                    ]
        out_ref[:, block] = result[block].reshape(devices, rows, LANES).astype(jnp.bfloat16)


def renew_kernel(got_ref, green_ref, sigma_hbm, renewed_hbm, stage, sigma, renewed, sems):
    local, _, _, order, _ = sigma.shape
    rows = got_ref.shape[2]
    depth = rows // local
    rest = order - LANES
    copies = []
    inner = []
    for energy in range(local):
        for block in range(3):
            stage[energy, block] = (
                got_ref[:, block, energy * depth : (energy + 1) * depth]
                .astype(jnp.float32)
                .reshape(2 * order, LANES)
            )
        for part in range(2):
            at = pl.ds(part, order, stride=2)
            mixed = stage[energy, 2, at, :]
            sigma[energy, 0, part, :, :LANES] = stage[energy, 0, at, :].astype(jnp.bfloat16)
            sigma[energy, 1, part, :, :LANES] = stage[energy, 1, at, :].astype(jnp.bfloat16)
            sigma[energy, 0, part, :, LANES:] = mixed[:, :rest].astype(jnp.bfloat16)
            sigma[energy, 1, part, :, LANES:] = pltpu.roll(mixed, rest, 1)[:, :rest].astype(jnp.bfloat16)
        copies.append(pltpu.make_async_copy(sigma.at[energy], sigma_hbm.at[energy], sems.at[energy, 0]))
        copies[-1].start()
        inner.append([inner_parts(green_ref[energy, slab, 0], sigma[energy, slab]) for slab in range(2)])
    for energy in range(local):
        for slab in range(2):
            fresh = outer_parts(green_ref[energy, slab, 0], inner[energy][slab])
            for part in range(2):
                renewed[energy, slab, part] = fresh[part].astype(jnp.bfloat16)
            copies.append(
                pltpu.make_async_copy(
                    renewed.at[energy, slab], renewed_hbm.at[energy, slab], sems.at[energy, 1 + slab]
                )
            )
            copies[-1].start()
    for copy in copies:
        copy.wait()


def split_high_low(matrix):
    high = matrix.astype(ml_dtypes.bfloat16)
    low = (matrix - high.astype(np.float64)).astype(ml_dtypes.bfloat16)
    return jnp.asarray(np.concatenate([high, low], axis=1))


def transforms(energies, devices):
    local = energies // devices
    index = np.arange(energies)
    angle = (index[:, None] * index[None, :] % energies) * (2.0 * math.pi / energies)
    cosine, sine = np.cos(angle), np.sin(angle)
    order = (np.arange(devices)[None, :] * local + np.arange(local)[:, None]).reshape(-1)
    scale = 1.0 / (energies * math.sqrt(energies))
    forward = np.block([[cosine[:, order], sine[:, order]], [-sine[:, order], cosine[:, order]]])
    backward = scale * np.block([[cosine[order], -sine[order]], [sine[order], cosine[order]]])
    plain = np.stack([np.stack([cosine, sine], 1), np.stack([-sine, cosine], 1)])
    return split_high_low(forward), split_high_low(backward), jnp.asarray(plain, jnp.float32)


def vmem(array):
    return pltpu.with_memory_space_constraint(array, pltpu.VMEM)


def hbm(array):
    return pltpu.with_memory_space_constraint(array, pltpu.HBM)


IN_VMEM = pl.BlockSpec(memory_space=pltpu.VMEM)
IN_HBM = pl.BlockSpec(memory_space=pltpu.HBM)
GRANT = pltpu.CompilerParams(vmem_limit_bytes=20 << 20)


def fast_shards(green_ret, sigma_less, screened):
    devices = lax.axis_size("energy")
    local, slabs, _, order, _ = sigma_less.shape
    energies = local * devices
    owned = order // devices
    depth = 2 * owned
    rows = depth * local
    sent = pltpu.VMEM((devices, 3, rows, LANES), jnp.bfloat16)
    dma = pltpu.SemaphoreType.DMA

    halo = lax.ppermute(sigma_less, "slab", [(0, 1), (1, 0)])
    total, edge = pl.pallas_call(
        near_kernel,
        out_shape=(
            pltpu.VMEM((local, slabs, 2, order, order), jnp.float32),
            pltpu.VMEM((local, 2, order, order), jnp.bfloat16),
        ),
        in_specs=[IN_HBM, IN_HBM],
        out_specs=(IN_VMEM, IN_VMEM),
        scratch_shapes=[
            pltpu.VMEM((local, slabs, 2, 2, order, order), jnp.bfloat16),
            pltpu.VMEM((local, slabs, 2, order, order), jnp.bfloat16),
            dma((local, 4)),
        ],
        compiler_params=GRANT,
        name="near",
    )(hbm(green_ret), hbm(sigma_less))
    send = pl.pallas_call(
        far_kernel,
        out_shape=sent,
        in_specs=[IN_VMEM] * 3,
        out_specs=IN_VMEM,
        scratch_shapes=[pltpu.VMEM((local, 3, 2 * order, LANES), jnp.float32)],
        compiler_params=GRANT,
        name="far",
    )(vmem(total), vmem(edge), vmem(halo))
    got = lax.all_to_all(send, "energy", split_axis=0, concat_axis=0, tiled=True)

    forward, backward, plain = transforms(energies, devices)
    grid_w = screened.reshape(energies, slabs, 2, owned, order)
    head, tail = grid_w[..., :LANES], grid_w[..., LANES:]
    arranged = jnp.stack([head[:, 0], head[:, 1], jnp.concatenate([tail[:, 0], tail[:, 1]], axis=-1)])
    arranged = arranged.reshape(3, energies, 2, owned * LANES)
    what = jnp.einsum("pfqe,keqn->kpfn", plain, arranged, precision=lax.Precision.HIGH)
    what = what.reshape(3, 2 * energies, owned * LANES)

    fresh = pl.pallas_call(
        convolve_kernel,
        out_shape=sent,
        in_specs=[IN_VMEM] * 4,
        out_specs=IN_VMEM,
        scratch_shapes=[
            pltpu.VMEM((3, devices * rows, LANES), jnp.float32),
            pltpu.VMEM((3, devices * rows, LANES), jnp.float32),
        ],
        compiler_params=GRANT,
        name="convolve",
    )(vmem(got), vmem(what), vmem(forward), vmem(backward))
    back = lax.all_to_all(fresh, "energy", split_axis=0, concat_axis=0, tiled=True)

    out = jax.ShapeDtypeStruct((local, slabs, 2, order, order), jnp.bfloat16)
    return pl.pallas_call(
        renew_kernel,
        out_shape=(out, out),
        in_specs=[IN_VMEM] * 2,
        out_specs=(IN_HBM, IN_HBM),
        scratch_shapes=[
            pltpu.VMEM((local, 3, 2 * order, LANES), jnp.float32),
            pltpu.VMEM((local, slabs, 2, order, order), jnp.bfloat16),
            pltpu.VMEM((local, slabs, 2, order, order), jnp.bfloat16),
            dma((local, 3)),
        ],
        compiler_params=GRANT,
        name="renew",
    )(vmem(back), vmem(green_ret[:, :, 1:2]))


def with_halo(cells, sides, width):
    for axis, dim in sides:
        count = lax.axis_size(axis)
        ends = count - 1
        head = lax.slice_in_dim(cells, 0, width, axis=dim)
        tail = lax.slice_in_dim(cells, cells.shape[dim] - width, cells.shape[dim], axis=dim)
        cells = jnp.concatenate(
            [
                lax.ppermute(tail, axis, [(i, (i + 1) % count) for i in range(ends)]),
                cells,
                lax.ppermute(head, axis, [((i + 1) % count, i) for i in range(ends)]),
            ],
            axis=dim,
        )
    return cells


def cmul_adj(left, right):
    lr = left[..., 0, :, :]
    li = left[..., 1, :, :]
    rr = right[..., 0, :, :]
    ri = right[..., 1, :, :]
    real = jnp.einsum(
        "...ab,...cb->...ac", lr, rr, preferred_element_type=jnp.float32
    ) + jnp.einsum("...ab,...cb->...ac", li, ri, preferred_element_type=jnp.float32)
    imag = jnp.einsum(
        "...ab,...cb->...ac", li, rr, preferred_element_type=jnp.float32
    ) - jnp.einsum("...ab,...cb->...ac", lr, ri, preferred_element_type=jnp.float32)
    return jnp.stack([real, imag], axis=-3)


def cmul_plain(left, right):
    lr = left[..., 0, :, :]
    li = left[..., 1, :, :]
    rr = right[..., 0, :, :]
    ri = right[..., 1, :, :]
    real = jnp.einsum(
        "...ab,...bc->...ac", lr, rr, preferred_element_type=jnp.float32
    ) - jnp.einsum("...ab,...bc->...ac", li, ri, preferred_element_type=jnp.float32)
    imag = jnp.einsum(
        "...ab,...bc->...ac", lr, ri, preferred_element_type=jnp.float32
    ) + jnp.einsum("...ab,...bc->...ac", li, rr, preferred_element_type=jnp.float32)
    return jnp.stack([real, imag], axis=-3)


def convolve(owned, interaction):
    energies = owned.shape[0]
    index = jnp.arange(energies, dtype=jnp.int32)
    phase = index[:, None] * index[None, :] % energies
    angle = phase.astype(jnp.float32) * (2.0 * math.pi / energies)
    cosine = jnp.cos(angle)
    sine = jnp.sin(angle)
    forward = jnp.stack(
        [jnp.stack([cosine, sine], axis=1), jnp.stack([-sine, cosine], axis=1)], axis=0
    )
    backward = jnp.stack(
        [jnp.stack([cosine, -sine], axis=1), jnp.stack([sine, cosine], axis=1)], axis=0
    )
    ghat = jnp.einsum(
        "pfqe,esqn->pfsn", forward, owned.astype(jnp.float32), precision=lax.Precision.HIGH
    )
    what = jnp.einsum("pfqe,esqn->pfsn", forward, interaction, precision=lax.Precision.HIGH)
    prod_real = ghat[0] * what[0] - ghat[1] * what[1]
    prod_imag = ghat[0] * what[1] + ghat[1] * what[0]
    product = jnp.stack([prod_real, prod_imag], axis=0)
    result = jnp.einsum("pfqe,qesn->fspn", backward, product, precision=lax.Precision.HIGH)
    result = result * (1.0 / (energies * math.sqrt(energies)))
    return result.astype(jnp.bfloat16)


def plain_shards(green_ret, sigma_less, screened):
    energy_dev = sigma_less.shape[0]
    slab_dev = sigma_less.shape[1]
    order = sigma_less.shape[-1]
    padded = with_halo(sigma_less, (("slab", 1),), 1)
    total = None
    for k in range(3):
        coupling = green_ret[:, :, k]
        inner = cmul_adj(padded[:, k : k + slab_dev], coupling).astype(jnp.bfloat16)
        term = cmul_plain(coupling, inner)
        total = term if total is None else total + term
    lesser = total.astype(jnp.bfloat16).reshape(energy_dev, slab_dev, 2, order * order)
    owned = lax.all_to_all(lesser, "energy", split_axis=3, concat_axis=0, tiled=True)
    fresh = convolve(owned, screened)
    sigma_new = lax.all_to_all(fresh, "energy", split_axis=0, concat_axis=3, tiled=True)
    sigma_new = sigma_new.reshape(energy_dev, slab_dev, 2, order, order)
    diag = green_ret[:, :, 1]
    inner = cmul_adj(sigma_new, diag).astype(jnp.bfloat16)
    renewed = cmul_plain(diag, inner).astype(jnp.bfloat16)
    return (sigma_new, renewed)


def shards(green_ret, sigma_less, screened):
    order = sigma_less.shape[-1]
    devices = lax.axis_size("energy")
    fits = (
        lax.axis_size("slab") == 2
        and sigma_less.shape[1] == 2
        and order == LANES + LANES // 2
        and order % devices == 0
        and (2 * order // devices) % 8 == 0
        and devices % 16 == 0
    )
    return (fast_shards if fits else plain_shards)(green_ret, sigma_less, screened)


def solution(mesh):
    in_specs = (
        P("energy", "slab", None, None, None, None),
        P("energy", "slab", None, None, None),
        P(None, "slab", None, "energy"),
    )
    out_specs = (P("energy", "slab", None, None, None), P("energy", "slab", None, None, None))
    return jax.shard_map(shards, mesh=mesh, in_specs=in_specs, out_specs=out_specs, check_vma=False)
```

```python
import functools
import math

import jax
import jax.numpy as jnp
import ml_dtypes
import numpy as np
from jax import lax
from jax.experimental import pallas as pl
from jax.experimental.pallas import tpu as pltpu
from jax.sharding import PartitionSpec as P

LANES = 128
NT = (((1,), (1,)), ((), ()))
NN = (((1,), (0,)), ((), ()))


def dot(left, right, dims):
    return lax.dot_general(left, right, dims, preferred_element_type=jnp.float32)


def inner_parts(green, sigma):
    real = dot(sigma[0], green[0], NT) + dot(sigma[1], green[1], NT)
    imag = dot(sigma[1], green[0], NT) + dot(sigma[0], -green[1], NT)
    return real.astype(jnp.bfloat16), imag.astype(jnp.bfloat16)


def outer_parts(green, inner):
    real, imag = inner
    return (
        dot(green[0], real, NN) + dot(-green[1], imag, NN),
        dot(green[0], imag, NN) + dot(green[1], real, NN),
    )


def congruence(green, sigma):
    return outer_parts(green, inner_parts(green, sigma))


def edge_place(slab_axis):
    first = lax.axis_index(slab_axis) == 0
    return jnp.where(first, 1, 0), jnp.where(first, 2, 0)


def near_kernel(green_hbm, sigma_hbm, total_ref, edge_ref, green, sigma, sems):
    local = green.shape[0]
    edge_slab, edge_block = edge_place("slab")
    copies = []
    for energy in range(local):
        copies.append(
            [
                pltpu.make_async_copy(sigma_hbm.at[energy], sigma.at[energy], sems.at[energy, 0]),
                pltpu.make_async_copy(
                    green_hbm.at[energy, 0, pl.ds(1, 2)], green.at[energy, 0], sems.at[energy, 1]
                ),
                pltpu.make_async_copy(
                    green_hbm.at[energy, 1, pl.ds(0, 2)], green.at[energy, 1], sems.at[energy, 2]
                ),
            ]
        )
    edges = [
        pltpu.make_async_copy(
            green_hbm.at[energy, edge_slab, edge_block], edge_ref.at[energy], sems.at[energy, 3]
        )
        for energy in range(local)
    ]
    for group in copies:
        for copy in group:
            copy.start()
    for copy in edges:
        copy.start()
    order = green.shape[-1]
    rest = order - LANES
    for energy in range(local):
        for group in [copies[0]] if energy == 0 else copies[1:] if energy == 1 else []:
            for copy in group:
                copy.wait()
        inner = [[None, None], [None, None]]
        for source in range(2):
            with_real, with_imag = [], []
            for slab in range(2):
                real, imag = green[energy, slab, source, 0], green[energy, slab, source, 1]
                with_real += [real, -imag[LANES:], -imag[:LANES]]
                with_imag += [imag, real[LANES:], real[:LANES]]
            both = dot(sigma[energy, source, 0], jnp.concatenate(with_real, axis=0), NT) + dot(
                sigma[energy, source, 1], jnp.concatenate(with_imag, axis=0), NT
            )
            for slab in range(2):
                at = 2 * slab * order
                mixed = pltpu.roll(both[:, at + LANES : at + 2 * LANES], rest, 1)
                turned = jnp.concatenate(
                    [both[:, at + 2 * LANES : at + 3 * LANES], mixed[:, :rest]], axis=1
                )
                inner[slab][source] = (
                    both[:, at : at + order].astype(jnp.bfloat16),
                    turned.astype(jnp.bfloat16),
                )
        for slab in range(2):
            left = jnp.concatenate(
                [green[energy, slab, source, part] for source in range(2) for part in range(2)], axis=1
            )
            near, next_ = inner[slab]
            total_ref[energy, slab, 0] = dot(
                left, jnp.concatenate([near[0], -near[1], next_[0], -next_[1]], axis=0), NN
            )
            total_ref[energy, slab, 1] = dot(
                left, jnp.concatenate([near[1], near[0], next_[1], next_[0]], axis=0), NN
            )
    for copy in edges:
        copy.wait()


def far_kernel(total_ref, edge_ref, halo_ref, out_ref, stage):
    local, _, _, order, _ = total_ref.shape
    devices, blocks, rows, _ = out_ref.shape
    depth = rows // local
    edge_slab, _ = edge_place("slab")
    other = 1 - edge_slab
    inner = [inner_parts(edge_ref[energy], halo_ref[energy, other]) for energy in range(local)]
    for energy in range(local):
        far = outer_parts(edge_ref[energy], inner[energy])
        for part in range(2):
            one, two = [
                total_ref[energy, slab, part] + jnp.where(edge_slab == slab, far[part], 0.0)
                for slab in range(2)
            ]
            at = pl.ds(part, order, stride=2)
            stage[energy, 0, at, :] = one[:, :LANES]
            stage[energy, 1, at, :] = two[:, :LANES]
            stage[energy, 2, at, :] = jnp.concatenate([one[:, LANES:], two[:, LANES:]], axis=1)
        for block in range(blocks):
            out_ref[:, block, energy * depth : (energy + 1) * depth] = (
                stage[energy, block].reshape(devices, depth, LANES).astype(jnp.bfloat16)
            )


def convolve_kernel(got_ref, what_ref, fwd_ref, bwd_ref, out_ref, stage, result):
    devices, blocks, rows, _ = got_ref.shape
    half = fwd_ref.shape[0] // 2
    local = half // devices
    depth = rows // local
    owned = depth // 2
    width = 2

    def place(block, row, part, energy):
        return block, pl.ds(energy * depth + row * 2 + part, devices, stride=rows), slice(None)

    each = [(part, energy) for part in range(2) for energy in range(local)]
    for block in range(blocks):
        stage[block] = got_ref[:, block].astype(jnp.float32).reshape(devices * rows, LANES)
        for start in range(0, owned, width):
            held = jnp.concatenate(
                [
                    jnp.concatenate([stage[place(block, row, *at)] for at in each], axis=0)
                    for row in range(start, start + width)
                ],
                axis=1,
            ).astype(jnp.bfloat16)
            ghat = dot(fwd_ref[...], jnp.concatenate([held, held], axis=0), NN)
            what = what_ref[block, :, start * LANES : (start + width) * LANES]
            real = ghat[:half] * what[:half] - ghat[half:] * what[half:]
            imag = ghat[:half] * what[half:] + ghat[half:] * what[:half]
            product = jnp.concatenate([real, imag], axis=0).astype(jnp.bfloat16)
            fresh = dot(bwd_ref[...], jnp.concatenate([product, product], axis=0), NN)
            for offset in range(width):
                for index, at in enumerate(each):
                    result[place(block, start + offset, *at)] = fresh[
                        index * devices : (index + 1) * devices, offset * LANES : (offset + 1) * LANES
                    ]
        out_ref[:, block] = result[block].reshape(devices, rows, LANES).astype(jnp.bfloat16)


def renew_kernel(got_ref, green_ref, sigma_hbm, renewed_hbm, stage, sigma, renewed, sems):
    local, _, _, order, _ = sigma.shape
    rows = got_ref.shape[2]
    depth = rows // local
    rest = order - LANES
    copies = []
    inner = []
    for energy in range(local):
        for block in range(3):
            stage[energy, block] = (
                got_ref[:, block, energy * depth : (energy + 1) * depth]
                .astype(jnp.float32)
                .reshape(2 * order, LANES)
            )
        for part in range(2):
            at = pl.ds(part, order, stride=2)
            mixed = stage[energy, 2, at, :]
            sigma[energy, 0, part, :, :LANES] = stage[energy, 0, at, :].astype(jnp.bfloat16)
            sigma[energy, 1, part, :, :LANES] = stage[energy, 1, at, :].astype(jnp.bfloat16)
            sigma[energy, 0, part, :, LANES:] = mixed[:, :rest].astype(jnp.bfloat16)
            sigma[energy, 1, part, :, LANES:] = pltpu.roll(mixed, rest, 1)[:, :rest].astype(jnp.bfloat16)
        copies.append(pltpu.make_async_copy(sigma.at[energy], sigma_hbm.at[energy], sems.at[energy, 0]))
        copies[-1].start()
        inner.append([inner_parts(green_ref[energy, slab, 0], sigma[energy, slab]) for slab in range(2)])
    for energy in range(local):
        for slab in range(2):
            fresh = outer_parts(green_ref[energy, slab, 0], inner[energy][slab])
            for part in range(2):
                renewed[energy, slab, part] = fresh[part].astype(jnp.bfloat16)
            copies.append(
                pltpu.make_async_copy(
                    renewed.at[energy, slab], renewed_hbm.at[energy, slab], sems.at[energy, 1 + slab]
                )
            )
            copies[-1].start()
    for copy in copies:
        copy.wait()


def split_high_low(matrix):
    high = matrix.astype(ml_dtypes.bfloat16)
    low = (matrix - high.astype(np.float64)).astype(ml_dtypes.bfloat16)
    return jnp.asarray(np.concatenate([high, low], axis=1))


def transforms(energies, devices):
    local = energies // devices
    index = np.arange(energies)
    angle = (index[:, None] * index[None, :] % energies) * (2.0 * math.pi / energies)
    cosine, sine = np.cos(angle), np.sin(angle)
    order = (np.arange(devices)[None, :] * local + np.arange(local)[:, None]).reshape(-1)
    scale = 1.0 / (energies * math.sqrt(energies))
    forward = np.block([[cosine[:, order], sine[:, order]], [-sine[:, order], cosine[:, order]]])
    backward = scale * np.block([[cosine[order], -sine[order]], [sine[order], cosine[order]]])
    plain = np.stack([np.stack([cosine, sine], 1), np.stack([-sine, cosine], 1)])
    return split_high_low(forward), split_high_low(backward), jnp.asarray(plain, jnp.float32)


def vmem(array):
    return pltpu.with_memory_space_constraint(array, pltpu.VMEM)


def hbm(array):
    return pltpu.with_memory_space_constraint(array, pltpu.HBM)


IN_VMEM = pl.BlockSpec(memory_space=pltpu.VMEM)
IN_HBM = pl.BlockSpec(memory_space=pltpu.HBM)
GRANT = pltpu.CompilerParams(vmem_limit_bytes=20 << 20)


def fast_shards(green_ret, sigma_less, screened):
    devices = lax.axis_size("energy")
    local, slabs, _, order, _ = sigma_less.shape
    energies = local * devices
    owned = order // devices
    depth = 2 * owned
    rows = depth * local
    sent = pltpu.VMEM((devices, 3, rows, LANES), jnp.bfloat16)
    dma = pltpu.SemaphoreType.DMA

    halo = lax.ppermute(sigma_less, "slab", [(0, 1), (1, 0)])
    total, edge = pl.pallas_call(
        near_kernel,
        out_shape=(
            pltpu.VMEM((local, slabs, 2, order, order), jnp.float32),
            pltpu.VMEM((local, 2, order, order), jnp.bfloat16),
        ),
        in_specs=[IN_HBM, IN_HBM],
        out_specs=(IN_VMEM, IN_VMEM),
        scratch_shapes=[
            pltpu.VMEM((local, slabs, 2, 2, order, order), jnp.bfloat16),
            pltpu.VMEM((local, slabs, 2, order, order), jnp.bfloat16),
            dma((local, 4)),
        ],
        compiler_params=pltpu.CompilerParams(
            vmem_limit_bytes=20 << 20
        ),
        name="near",
    )(hbm(green_ret), hbm(sigma_less))
    send = pl.pallas_call(
        far_kernel,
        out_shape=sent,
        in_specs=[IN_VMEM] * 3,
        out_specs=IN_VMEM,
        scratch_shapes=[pltpu.VMEM((local, 3, 2 * order, LANES), jnp.float32)],
        compiler_params=pltpu.CompilerParams(
            vmem_limit_bytes=20 << 20
        ),
        name="far",
    )(vmem(total), vmem(edge), vmem(halo))
    got = lax.all_to_all(send, "energy", split_axis=0, concat_axis=0, tiled=True)

    forward, backward, plain = transforms(energies, devices)
    grid_w = screened.reshape(energies, slabs, 2, owned, order)
    head, tail = grid_w[..., :LANES], grid_w[..., LANES:]
    arranged = jnp.stack([head[:, 0], head[:, 1], jnp.concatenate([tail[:, 0], tail[:, 1]], axis=-1)])
    arranged = arranged.reshape(3, energies, 2, owned * LANES)
    what = jnp.einsum("pfqe,keqn->kpfn", plain, arranged, precision=lax.Precision.HIGH)
    what = what.reshape(3, 2 * energies, owned * LANES)

    fresh = pl.pallas_call(
        convolve_kernel,
        out_shape=sent,
        in_specs=[IN_VMEM] * 4,
        out_specs=IN_VMEM,
        scratch_shapes=[
            pltpu.VMEM((3, devices * rows, LANES), jnp.float32),
            pltpu.VMEM((3, devices * rows, LANES), jnp.float32),
        ],
        compiler_params=GRANT,
        name="convolve",
    )(vmem(got), vmem(what), vmem(forward), vmem(backward))
    back = lax.all_to_all(fresh, "energy", split_axis=0, concat_axis=0, tiled=True)

    out = jax.ShapeDtypeStruct((local, slabs, 2, order, order), jnp.bfloat16)
    return pl.pallas_call(
        renew_kernel,
        out_shape=(out, out),
        in_specs=[IN_VMEM] * 2,
        out_specs=(IN_HBM, IN_HBM),
        scratch_shapes=[
            pltpu.VMEM((local, 3, 2 * order, LANES), jnp.float32),
            pltpu.VMEM((local, slabs, 2, order, order), jnp.bfloat16),
            pltpu.VMEM((local, slabs, 2, order, order), jnp.bfloat16),
            dma((local, 3)),
        ],
        compiler_params=GRANT,
        name="renew",
    )(vmem(back), vmem(green_ret[:, :, 1:2]))


def with_halo(cells, sides, width):
    for axis, dim in sides:
        count = lax.axis_size(axis)
        ends = count - 1
        head = lax.slice_in_dim(cells, 0, width, axis=dim)
        tail = lax.slice_in_dim(cells, cells.shape[dim] - width, cells.shape[dim], axis=dim)
        cells = jnp.concatenate(
            [
                lax.ppermute(tail, axis, [(i, (i + 1) % count) for i in range(ends)]),
                cells,
                lax.ppermute(head, axis, [((i + 1) % count, i) for i in range(ends)]),
            ],
            axis=dim,
        )
    return cells


def cmul_adj(left, right):
    lr = left[..., 0, :, :]
    li = left[..., 1, :, :]
    rr = right[..., 0, :, :]
    ri = right[..., 1, :, :]
    real = jnp.einsum(
        "...ab,...cb->...ac", lr, rr, preferred_element_type=jnp.float32
    ) + jnp.einsum("...ab,...cb->...ac", li, ri, preferred_element_type=jnp.float32)
    imag = jnp.einsum(
        "...ab,...cb->...ac", li, rr, preferred_element_type=jnp.float32
    ) - jnp.einsum("...ab,...cb->...ac", lr, ri, preferred_element_type=jnp.float32)
    return jnp.stack([real, imag], axis=-3)


def cmul_plain(left, right):
    lr = left[..., 0, :, :]
    li = left[..., 1, :, :]
    rr = right[..., 0, :, :]
    ri = right[..., 1, :, :]
    real = jnp.einsum(
        "...ab,...bc->...ac", lr, rr, preferred_element_type=jnp.float32
    ) - jnp.einsum("...ab,...bc->...ac", li, ri, preferred_element_type=jnp.float32)
    imag = jnp.einsum(
        "...ab,...bc->...ac", lr, ri, preferred_element_type=jnp.float32
    ) + jnp.einsum("...ab,...bc->...ac", li, rr, preferred_element_type=jnp.float32)
    return jnp.stack([real, imag], axis=-3)


def convolve(owned, interaction):
    energies = owned.shape[0]
    index = jnp.arange(energies, dtype=jnp.int32)
    phase = index[:, None] * index[None, :] % energies
    angle = phase.astype(jnp.float32) * (2.0 * math.pi / energies)
    cosine = jnp.cos(angle)
    sine = jnp.sin(angle)
    forward = jnp.stack(
        [jnp.stack([cosine, sine], axis=1), jnp.stack([-sine, cosine], axis=1)], axis=0
    )
    backward = jnp.stack(
        [jnp.stack([cosine, -sine], axis=1), jnp.stack([sine, cosine], axis=1)], axis=0
    )
    ghat = jnp.einsum(
        "pfqe,esqn->pfsn", forward, owned.astype(jnp.float32), precision=lax.Precision.HIGH
    )
    what = jnp.einsum("pfqe,esqn->pfsn", forward, interaction, precision=lax.Precision.HIGH)
    prod_real = ghat[0] * what[0] - ghat[1] * what[1]
    prod_imag = ghat[0] * what[1] + ghat[1] * what[0]
    product = jnp.stack([prod_real, prod_imag], axis=0)
    result = jnp.einsum("pfqe,qesn->fspn", backward, product, precision=lax.Precision.HIGH)
    result = result * (1.0 / (energies * math.sqrt(energies)))
    return result.astype(jnp.bfloat16)


def plain_shards(green_ret, sigma_less, screened):
    energy_dev = sigma_less.shape[0]
    slab_dev = sigma_less.shape[1]
    order = sigma_less.shape[-1]
    padded = with_halo(sigma_less, (("slab", 1),), 1)
    total = None
    for k in range(3):
        coupling = green_ret[:, :, k]
        inner = cmul_adj(padded[:, k : k + slab_dev], coupling).astype(jnp.bfloat16)
        term = cmul_plain(coupling, inner)
        total = term if total is None else total + term
    lesser = total.astype(jnp.bfloat16).reshape(energy_dev, slab_dev, 2, order * order)
    owned = lax.all_to_all(lesser, "energy", split_axis=3, concat_axis=0, tiled=True)
    fresh = convolve(owned, screened)
    sigma_new = lax.all_to_all(fresh, "energy", split_axis=0, concat_axis=3, tiled=True)
    sigma_new = sigma_new.reshape(energy_dev, slab_dev, 2, order, order)
    diag = green_ret[:, :, 1]
    inner = cmul_adj(sigma_new, diag).astype(jnp.bfloat16)
    renewed = cmul_plain(diag, inner).astype(jnp.bfloat16)
    return (sigma_new, renewed)


def shards(green_ret, sigma_less, screened):
    order = sigma_less.shape[-1]
    devices = lax.axis_size("energy")
    fits = (
        lax.axis_size("slab") == 2
        and sigma_less.shape[1] == 2
        and order == LANES + LANES // 2
        and order % devices == 0
        and (2 * order // devices) % 8 == 0
        and devices % 16 == 0
    )
    return (fast_shards if fits else plain_shards)(green_ret, sigma_less, screened)


def solution(mesh):
    in_specs = (
        P("energy", "slab", None, None, None, None),
        P("energy", "slab", None, None, None),
        P(None, "slab", None, "energy"),
    )
    out_specs = (P("energy", "slab", None, None, None), P("energy", "slab", None, None, None))
    return jax.shard_map(shards, mesh=mesh, in_specs=in_specs, out_specs=out_specs, check_vma=False)
```
